32 devices in a mesh: slab: 2 (over y), bx: 8 (over z, x), by: 2 (over core).
Axes of the slice: x: 2, y: 2, z: 4, core: 2. Of those that a mesh axis runs over, the one named last changes fastest.
Arguments:
- phi: float32 [64, 128, 2048], P('slab', 'bx', 'by'), parts along dimension 0, may hold values from -6 to 6
- first_measurement: float32 [128, 2048], P('slab', 'by'), parts along dimension 0, may hold values from 0.5 to 3.5
- second_measurement: float32 [128, 128], P('slab', 'bx'), parts along dimension 0, may hold values from 0.5 to 3.5
- first_view_mask: int32 [128, 2048], P('slab', 'by'), parts along dimension 0, may hold values 0 or 1
- second_view_mask: int32 [128, 128], P('slab', 'bx'), parts along dimension 0, may hold values 0 or 1
- plane_detector_rows: int32 [32], replicated, may hold values from 0 to 63, as said below
Outputs:
- gradient: float32 [64, 128, 2048], P('slab', 'bx', 'by'), parts along dimension 0
The draws below stay inside these ranges and needn't reach their ends.
There are 2 independent parts, one for each index of `slab`. The reference program is written for one: setup_inputs(seed, part) draws one part's arguments, and reference() takes and returns one part's arrays. A program takes and returns all parts, laid end to end along the dimension named above; an argument that names none is the same for every part. Nothing has to cross between parts.
Inputs may be any that keep to these rules, and one draw needn't show every extreme that they name: `plane_detector_rows`: plane z reads detector row 2 z or 2 z + 1; plane 0 reads row 0 and the last plane reads row 63.
All inputs are finite; a program needn't handle non-finite values. No bound on the sum of `first_view_mask` or of `second_view_mask` on one device may be relied on, other than what follows from the above.
Results may differ from the reference program's by a relative error of at most 0.00002.
Values sent between devices are 32-bit elements; how exact they have to be, the bound alone decides.
A program may use at most 64 MiB of HBM per device.

```python
import jax
import jax.numpy as jnp
from jax import lax

CZ = 32
CELLS_FIRST = 128
CELLS_SECOND = 2048
DETECTOR_ROWS = 64


def draw_phi(key, part):
    key_noise = jax.random.fold_in(key, 11)
    key_shift = jax.random.fold_in(key, 12)
    shift = jax.random.uniform(key_shift, (CZ, CELLS_FIRST, 1), jnp.float32, -1.5, 1.5)
    values = jax.random.normal(key_noise, (CZ, CELLS_FIRST, CELLS_SECOND), jnp.float32) + shift
    return jnp.clip(values, -6.0, 6.0)


def draw_plane_detector_rows(key, part):
    bits = jax.random.randint(jax.random.fold_in(key, 21), (CZ,), 0, 2)
    planes = jnp.arange(CZ, dtype=jnp.int32)
    bits = jnp.where(planes == 0, 0, jnp.where(planes == CZ - 1, 1, bits))
    return (2 * planes + bits).astype(jnp.int32)


def place_ends(values, own_key, least, high):
    longest = values.shape.index(max(values.shape))
    spots = []
    for shift in (0, 1):
        where = [jax.random.randint(jax.random.fold_in(own_key, axis), (), 0, length) for axis, length in enumerate(values.shape)]
        where[longest] = (where[longest] + shift) % values.shape[longest]
        spots.append(tuple(where))
    return values.at[spots[0]].set(least).at[spots[1]].set(high)


def shard_levels(key, dims, cuts, smallest, largest):
    level = 1.0
    for dim, parts in cuts:
        steps = jax.random.uniform(jax.random.fold_in(jax.random.fold_in(key, 6), dim), (parts,), jnp.float32, smallest / len(cuts), largest / len(cuts))
        level = level * jnp.repeat(jnp.exp(steps), dims[dim] // parts).reshape((-1,) + (1,) * (len(dims) - 1 - dim))
    return level


def setup_inputs(seed: int = 0, part: int = 0) -> dict:
    streams_of = jax.random.split(jax.random.key(seed), 7)
    part_keys = jax.random.split(jax.random.fold_in(streams_of[6], part), 7)
    phi = draw_phi(jax.random.fold_in(jax.random.fold_in(streams_of[6], part), 71), part)
    first_measurement = jnp.clip(0.5 + 3.0 * jax.random.uniform(part_keys[1], (DETECTOR_ROWS, CELLS_SECOND), jnp.float32) ** shard_levels(part_keys[1], (DETECTOR_ROWS, CELLS_SECOND), ((1, 2),), -0.2, 0.2), 0.5, 3.5)
    second_measurement = jnp.clip(0.5 + 3.0 * jax.random.uniform(part_keys[2], (DETECTOR_ROWS, CELLS_FIRST), jnp.float32) ** shard_levels(part_keys[2], (DETECTOR_ROWS, CELLS_FIRST), ((1, 8),), -0.2, 0.2), 0.5, 3.5)
    first_view_mask = place_ends((jax.random.randint(part_keys[3], (DETECTOR_ROWS, CELLS_SECOND), 0, 4) < 3).astype(jnp.int32), jax.random.fold_in(part_keys[3], 1), 0, 1)
    second_view_mask = place_ends((jax.random.randint(part_keys[4], (DETECTOR_ROWS, CELLS_FIRST), 0, 4) < 3).astype(jnp.int32), jax.random.fold_in(part_keys[4], 1), 0, 1)
    plane_detector_rows = draw_plane_detector_rows(jax.random.fold_in(streams_of[6], 71), part)
    return dict(phi=phi, first_measurement=first_measurement, second_measurement=second_measurement, first_view_mask=first_view_mask, second_view_mask=second_view_mask, plane_detector_rows=plane_detector_rows)


LAMBDA = 0.5
BETA2 = 1.0

def curvature_of(padded):
    core = padded[:-1, :-1, :-1]
    grad_z = padded[1:, :-1, :-1] - core
    grad_x = padded[:-1, 1:, :-1] - core
    grad_y = padded[:-1, :-1, 1:] - core
    magnitude = jnp.sqrt(grad_z * grad_z + grad_x * grad_x + grad_y * grad_y + BETA2)
    flux_z = grad_z / magnitude
    flux_x = grad_x / magnitude
    flux_y = grad_y / magnitude
    div_z = flux_z[1:, 1:, 1:] - flux_z[:-1, 1:, 1:]
    div_x = flux_x[1:, 1:, 1:] - flux_x[1:, :-1, 1:]
    div_y = flux_y[1:, 1:, 1:] - flux_y[1:, 1:, :-1]
    return div_z + div_x + div_y

def reference(phi, first_measurement, second_measurement, first_view_mask, second_view_mask, plane_detector_rows):
    tanh_phi = jnp.tanh(phi)
    heav = 0.5 * (1.0 + tanh_phi)
    slope = 0.5 * (1.0 - tanh_phi * tanh_phi)
    first_projection = lax.optimization_barrier(jnp.sum(heav, axis=1)) * (4.0 / CELLS_FIRST)
    second_projection = lax.optimization_barrier(jnp.sum(heav, axis=2)) * (4.0 / CELLS_SECOND)
    first_residual = first_view_mask[plane_detector_rows].astype(jnp.float32) * (first_projection - first_measurement[plane_detector_rows])
    second_residual = second_view_mask[plane_detector_rows].astype(jnp.float32) * (second_projection - second_measurement[plane_detector_rows])
    curv = curvature_of(jnp.pad(phi, 1))
    return slope * (first_residual[:, None, :] + second_residual[:, :, None]) - LAMBDA * curv
```

```python
import functools

import jax
import jax.numpy as jnp
from jax import lax
from jax.experimental import pallas as pl
from jax.experimental.pallas import tpu as pltpu
from jax.sharding import PartitionSpec as P

LAMBDA = 0.5
BETA2 = 1.0
TILE = 128
GROUP = 8
MESH = pl.DeviceIdType.MESH


def exchange_kernel(
    n, phi_hbm, ma_hbm, mb_hbm, va_hbm, vb_hbm, rows_hbm,
    base_hbm, ra_hbm, rb_hbm,
    ext, out, esend_recv, sums, rs_recv, pieces, ra_out, bsum, bsum_recv, rb,
    x_first, x_last, h_next, h_prev, corner, flux_prev,
    ma, va, mb, vb, rows,
    in_sem, small_sem, out_sem, fin_sem,
    rs_send, rs_sem, ag_send, ag_sem, pair_send, pair_sem, halo_send, halo_sem,
):
    planes, cells_x, cells_y = phi_hbm.shape
    groups = planes // GROUP
    me = lax.axis_index("bx")
    half = lax.axis_index("by")
    other = 1 - half
    total_x = cells_x * n
    total_y = cells_y * 2

    barrier = pltpu.get_barrier_semaphore()
    for k in range(1, n):
        pl.semaphore_signal(barrier, inc=1, device_id={"bx": lax.rem(me + k, n)}, device_id_type=MESH)
    for k in range(n):
        pl.semaphore_signal(
            barrier, inc=1, device_id={"bx": lax.rem(me + k, n), "by": other}, device_id_type=MESH
        )

    def load(g):
        return pltpu.make_async_copy(
            phi_hbm.at[pl.ds(g * GROUP, GROUP)],
            ext.at[pl.ds(g * GROUP, GROUP), :, pl.ds(TILE, cells_y)],
            in_sem.at[g],
        )

    for g in range(groups):
        load(g).start()
    lanes_me = pl.ds(pl.multiple_of(me * TILE, TILE), TILE)
    small = [
        pltpu.make_async_copy(ma_hbm.at[:, lanes_me], ma, small_sem.at[0]),
        pltpu.make_async_copy(va_hbm.at[:, lanes_me], va, small_sem.at[1]),
        pltpu.make_async_copy(mb_hbm, mb, small_sem.at[2]),
        pltpu.make_async_copy(vb_hbm, vb, small_sem.at[3]),
        pltpu.make_async_copy(rows_hbm, rows, small_sem.at[4]),
    ]
    for copy in small:
        copy.start()

    for g in range(groups):
        load(g).wait()

        def first_pass(c, _, g=g):
            at = pl.ds(g * GROUP, GROUP)
            cells = ext[at, :, pl.ds(pl.multiple_of(TILE + c * TILE, TILE), TILE)]
            t = jnp.tanh(cells)
            sums[c, at, :] = jnp.sum(t, axis=1)
            cols = pl.ds(pl.multiple_of(c * TILE, TILE), TILE)
            x_first[at, cols] = cells[:, 0, :]
            x_last[at, cols] = cells[:, cells_x - 1, :]
            return _ + t

        bsum[pl.ds(g * GROUP, GROUP)] = lax.fori_loop(
            0, n, first_pass, jnp.zeros((GROUP, cells_x, TILE), jnp.float32)
        )

    pl.semaphore_wait(barrier, 2 * n - 1)

    def scatter(k):
        to = lax.rem(me + k, n)
        return pltpu.make_async_remote_copy(
            src_ref=sums.at[to], dst_ref=rs_recv.at[n - k], send_sem=rs_send.at[k],
            recv_sem=rs_sem.at[n - k], device_id={"bx": to}, device_id_type=MESH,
        )

    def gather(k):
        to = lax.rem(me + k, n)
        return pltpu.make_async_remote_copy(
            src_ref=pieces.at[me], dst_ref=pieces.at[me], send_sem=ag_send.at[k],
            recv_sem=ag_sem.at[n - k], device_id={"bx": to}, device_id_type=MESH,
        )

    def pair(i):
        edge = pl.ds(pl.multiple_of(TILE + other * (cells_y - TILE), TILE), TILE)
        src, dst = ((ext.at[pl.ds(0, planes), :, edge], esend_recv), (bsum, bsum_recv))[i]
        return pltpu.make_async_remote_copy(
            src_ref=src, dst_ref=dst, send_sem=pair_send.at[i], recv_sem=pair_sem.at[i],
            device_id={"by": other}, device_id_type=MESH,
        )

    def to_next():
        return pltpu.make_async_remote_copy(
            src_ref=x_last, dst_ref=h_prev, send_sem=halo_send.at[0], recv_sem=halo_sem.at[0],
            device_id={"bx": lax.rem(me + 1, n)}, device_id_type=MESH,
        )

    def to_prev():
        return pltpu.make_async_remote_copy(
            src_ref=x_first, dst_ref=h_next, send_sem=halo_send.at[1], recv_sem=halo_sem.at[1],
            device_id={"bx": lax.rem(me + n - 1, n)}, device_id_type=MESH,
        )

    def corner_prev():
        return pltpu.make_async_remote_copy(
            src_ref=x_first.at[:, pl.ds(cells_y - TILE, TILE)], dst_ref=corner,
            send_sem=halo_send.at[2], recv_sem=halo_sem.at[2],
            device_id={"bx": lax.rem(me + n - 1, n), "by": other}, device_id_type=MESH,
        )

    def corner_next():
        return pltpu.make_async_remote_copy(
            src_ref=x_last.at[:, pl.ds(0, TILE)], dst_ref=corner,
            send_sem=halo_send.at[2], recv_sem=halo_sem.at[2],
            device_id={"bx": lax.rem(me + 1, n), "by": other}, device_id_type=MESH,
        )

    has_next = me < n - 1
    has_prev = me > 0
    for k in range(1, n):
        scatter(k).start()
    for i in range(2):
        pair(i).start()

    @pl.when(has_next)
    def _():
        to_next().start()

    @pl.when(has_prev)
    def _():
        to_prev().start()

    @pl.when(jnp.logical_and(has_prev, half == 0))
    def _():
        corner_prev().start()

    @pl.when(jnp.logical_and(has_next, half == 1))
    def _():
        corner_next().start()

    for copy in small:
        copy.wait()
    own = lax.broadcasted_iota(jnp.int32, (planes, planes), 0)
    across = lax.broadcasted_iota(jnp.int32, (planes, planes), 1)
    offsets = (rows[...] - 2 * across).astype(jnp.float32)
    odd = jnp.sum(jnp.where(own == across, offsets, 0.0), axis=1, keepdims=True) > 0.5

    def rows_of(ref):
        low = ref[pl.ds(0, planes, stride=2), :].astype(jnp.float32)
        high = ref[pl.ds(1, planes, stride=2), :].astype(jnp.float32)
        return jnp.where(odd, high, low)

    measured_a = rows_of(ma)
    mask_a = rows_of(va)
    measured_b = jnp.transpose(rows_of(mb))
    mask_b = jnp.transpose(rows_of(vb))

    total = sums[me]
    for k in range(1, n):
        scatter(n - k).wait_recv()
        total = total + rs_recv[k]
    pieces[me] = mask_a * ((2.0 + (2.0 / total_x) * total) - measured_a)
    for k in range(1, n):
        gather(k).start()

    pair(0).wait_recv()
    pair(1).wait_recv()
    column = lax.broadcasted_iota(jnp.int32, (cells_x, planes), 1)

    def second_view(z, _):
        pick = column == z
        both = jnp.sum(bsum[z] + bsum_recv[z], axis=1, keepdims=True)
        meas = jnp.sum(jnp.where(pick, measured_b, 0.0), axis=1, keepdims=True)
        mask = jnp.sum(jnp.where(pick, mask_b, 0.0), axis=1, keepdims=True)
        res = mask * ((2.0 + (2.0 / total_y) * both) - meas)
        rb[z] = jnp.broadcast_to(res, (cells_x, TILE))
        return _

    lax.fori_loop(0, planes, second_view, 0)
    rb_copy = pltpu.make_async_copy(rb, rb_hbm, fin_sem.at[0])
    rb_copy.start()

    lane3 = lax.broadcasted_iota(jnp.int32, (GROUP, cells_x, TILE), 2)
    keep3 = lane3 == half * (TILE - 1)
    for g in range(groups):
        at = pl.ds(g * GROUP, GROUP)
        ext[at, :, pl.ds(0, TILE)] = jnp.where(keep3, esend_recv[at], 0.0)
    ext[planes] = jnp.zeros((cells_x, cells_y + TILE), jnp.float32)

    @pl.when(has_prev)
    def _():
        to_next().wait_recv()

    @pl.when(jnp.logical_not(has_prev))
    def _():
        h_prev[...] = jnp.zeros_like(h_prev)

    @pl.when(has_next)
    def _():
        to_prev().wait_recv()

    @pl.when(jnp.logical_not(has_next))
    def _():
        h_next[...] = jnp.zeros_like(h_next)

    has_corner = jnp.logical_or(
        jnp.logical_and(has_prev, half == 0), jnp.logical_and(has_next, half == 1)
    )

    @pl.when(has_corner)
    def _():
        corner_prev().wait_recv()

    @pl.when(jnp.logical_not(has_corner))
    def _():
        corner[...] = jnp.zeros_like(corner)

    lane2 = lax.broadcasted_iota(jnp.int32, (planes, TILE), 1)
    corners = jnp.where(lane2 == half * (TILE - 1), corner[...], 0.0)
    width = cells_y + TILE
    before = jnp.concatenate([corners, h_prev[...]], axis=1)
    first = jnp.concatenate([jnp.zeros((planes, TILE), jnp.float32), x_first[...]], axis=1)
    above = pltpu.roll(before, planes - 1, axis=0)
    level = lax.broadcasted_iota(jnp.int32, (planes, width), 0)
    gz = jnp.where(level == planes - 1, 0.0, above) - before
    gx = first - before
    gy = pltpu.roll(before, width - 1, axis=1) - before
    flux_prev[...] = LAMBDA * gx * lax.rsqrt(gz * gz + gx * gx + gy * gy + BETA2)

    row = lax.broadcasted_iota(jnp.int32, (cells_x, width), 0)

    def curvature(z, flux_z_before):
        cells = ext[z]
        beyond = jnp.concatenate(
            [jnp.where(lane2[:1] == half * (TILE - 1), corner[pl.ds(z, 1), :], 0.0), h_next[pl.ds(z, 1), :]],
            axis=1,
        )
        right = jnp.where(row == cells_x - 1, beyond, pltpu.roll(cells, cells_x - 1, axis=0))
        gz = ext[z + 1] - cells
        gx = right - cells
        gy = pltpu.roll(cells, width - 1, axis=1) - cells
        scale = LAMBDA * lax.rsqrt(gz * gz + gx * gx + gy * gy + BETA2)
        fz = gz * scale
        fx = gx * scale
        fy = gy * scale
        fx_before = jnp.where(row == 0, flux_prev[pl.ds(z, 1), :], pltpu.roll(fx, 1, axis=0))
        fy_before = pltpu.roll(fy, 1, axis=1)
        div = (fz - flux_z_before) + (fx - fx_before) + (fy - fy_before)
        out[z] = div[:, TILE:]
        return fz

    def store(g):
        at = pl.ds(g * GROUP, GROUP)
        return pltpu.make_async_copy(out.at[at], base_hbm.at[at], out_sem.at[g])

    flux_z = LAMBDA * ext[0] * lax.rsqrt(ext[0] * ext[0] + BETA2)
    for g in range(groups):
        flux_z = lax.fori_loop(g * GROUP, (g + 1) * GROUP, curvature, flux_z)
        store(g).start()

    for k in range(1, n):
        gather(k).wait_recv()
    for c in range(n):
        ra_out[:, c * TILE:(c + 1) * TILE] = pieces[c]
    ra_copy = pltpu.make_async_copy(ra_out, ra_hbm, fin_sem.at[1])
    ra_copy.start()

    for k in range(1, n):
        scatter(k).wait_send()
        gather(k).wait_send()
    pair(0).wait_send()
    pair(1).wait_send()

    @pl.when(has_next)
    def _():
        to_next().wait_send()

    @pl.when(has_prev)
    def _():
        to_prev().wait_send()

    @pl.when(jnp.logical_and(has_prev, half == 0))
    def _():
        corner_prev().wait_send()

    @pl.when(jnp.logical_and(has_next, half == 1))
    def _():
        corner_next().wait_send()

    for g in range(groups):
        store(g).wait()
    rb_copy.wait()
    ra_copy.wait()


def finish_kernel(phi, base, ra, rb, grad):
    planes, cells_x, cells_y = phi.shape
    for z in range(planes):
        for c in range(cells_y // TILE):
            cols = pl.ds(c * TILE, TILE)
            t = jnp.tanh(phi[z, :, cols])
            res = ra[pl.ds(z, 1), cols] + rb[z]
            grad[z, :, cols] = (0.5 - 0.5 * (t * t)) * res - base[z, :, cols]


def per_device_kernels(n, phi, ma, mb, va, vb, rows):
    planes, cells_x, cells_y = phi.shape
    f32 = jnp.float32
    dma = pltpu.SemaphoreType.DMA
    det = ma.shape[0]
    groups = planes // GROUP
    any_spec = pl.BlockSpec(memory_space=pl.ANY)
    vmem = lambda *shape: pltpu.VMEM(shape, f32)
    base, ra, rb = pl.pallas_call(
        functools.partial(exchange_kernel, n),
        out_shape=(
            jax.ShapeDtypeStruct(phi.shape, f32),
            jax.ShapeDtypeStruct((planes, cells_y), f32),
            jax.ShapeDtypeStruct((planes, cells_x, TILE), f32),
        ),
        in_specs=[any_spec] * 6,
        out_specs=(any_spec,) * 3,
        scratch_shapes=[
            vmem(planes + 1, cells_x, cells_y + TILE), vmem(planes, cells_x, cells_y),
            vmem(planes, cells_x, TILE),
            vmem(n, planes, TILE), vmem(n, planes, TILE), vmem(n, planes, TILE), vmem(planes, cells_y),
            vmem(planes, cells_x, TILE), vmem(planes, cells_x, TILE), vmem(planes, cells_x, TILE),
            vmem(planes, cells_y), vmem(planes, cells_y), vmem(planes, cells_y), vmem(planes, cells_y),
            vmem(planes, TILE), vmem(planes, cells_y + TILE),
            vmem(det, TILE), pltpu.VMEM((det, TILE), jnp.int32),
            vmem(det, cells_x), pltpu.VMEM((det, cells_x), jnp.int32),
            pltpu.VMEM((1, planes), jnp.int32),
            dma((groups,)), dma((5,)), dma((groups,)), dma((2,)),
            dma((n,)), dma((n,)), dma((n,)), dma((n,)), dma((2,)), dma((2,)), dma((3,)), dma((3,)),
        ],
        compiler_params=pltpu.CompilerParams(
            collective_id=0, has_side_effects=True, vmem_limit_bytes=24 << 20
        ),
    )(phi, ma, mb, va, vb, rows.reshape(1, planes))
    block = pl.BlockSpec((GROUP, cells_x, cells_y), lambda i: (i, 0, 0))
    return pl.pallas_call(
        finish_kernel,
        grid=(groups,),
        out_shape=jax.ShapeDtypeStruct(phi.shape, f32),
        in_specs=[
            block, block,
            pl.BlockSpec((GROUP, cells_y), lambda i: (i, 0)),
            pl.BlockSpec((GROUP, cells_x, TILE), lambda i: (i, 0, 0)),
        ],
        out_specs=block,
        compiler_params=pltpu.CompilerParams(vmem_limit_bytes=16 << 20),
    )(phi, base, ra, rb)


def extended(cells, sides, width):
    for axis, dim in sides:
        count = lax.axis_size(axis)
        ends = count - 1
        head = lax.slice_in_dim(cells, 0, width, axis=dim)
        tail = lax.slice_in_dim(cells, cells.shape[dim] - width, cells.shape[dim], axis=dim)
        cells = jnp.concatenate(
            [
                lax.ppermute(tail, axis, [(i, (i + 1) % count) for i in range(ends)]),
                cells,
                lax.ppermute(head, axis, [((i + 1) % count, i) for i in range(ends)]),
            ],
            axis=dim,
        )
    return cells


def curvature_of(padded):
    core = padded[:-1, :-1, :-1]
    grad_z = padded[1:, :-1, :-1] - core
    grad_x = padded[:-1, 1:, :-1] - core
    grad_y = padded[:-1, :-1, 1:] - core
    magnitude = jnp.sqrt(grad_z * grad_z + grad_x * grad_x + grad_y * grad_y + BETA2)
    flux_z = grad_z / magnitude
    flux_x = grad_x / magnitude
    flux_y = grad_y / magnitude
    div_z = flux_z[1:, 1:, 1:] - flux_z[:-1, 1:, 1:]
    div_x = flux_x[1:, 1:, 1:] - flux_x[1:, :-1, 1:]
    div_y = flux_y[1:, 1:, 1:] - flux_y[1:, 1:, :-1]
    return div_z + div_x + div_y


def per_device(
    phi,
    first_measurement,
    second_measurement,
    first_view_mask,
    second_view_mask,
    plane_detector_rows,
):
    planes, cells_x, cells_y = phi.shape
    n = lax.axis_size("bx")
    if lax.axis_size("by") == 2 and n * TILE == cells_y and planes % GROUP == 0:
        return per_device_kernels(
            n, phi, first_measurement, second_measurement, first_view_mask, second_view_mask,
            plane_detector_rows,
        )
    total_x = cells_x * lax.axis_size("bx")
    total_y = cells_y * lax.axis_size("by")
    tanh_phi = jnp.tanh(phi)
    heav = 0.5 * (1.0 + tanh_phi)
    slope = 0.5 * (1.0 - tanh_phi * tanh_phi)
    part_a = jnp.sum(heav, axis=1)
    part_b = jnp.sum(heav, axis=2)
    first_measured_rows = jnp.take(first_measurement, plane_detector_rows, axis=0)
    first_mask_rows = jnp.take(first_view_mask, plane_detector_rows, axis=0).astype(jnp.float32)
    second_measured_rows = jnp.take(second_measurement, plane_detector_rows, axis=0)
    second_mask_rows = jnp.take(second_view_mask, plane_detector_rows, axis=0).astype(jnp.float32)
    second_projection = lax.psum(part_b, "by") * (4.0 / total_y)
    second_residual = second_mask_rows * (second_projection - second_measured_rows)
    first_projection = lax.psum(part_a, "bx") * (4.0 / total_x)
    first_residual = first_mask_rows * (first_projection - first_measured_rows)
    padded = extended(phi, (("bx", 1), ("by", 2)), 1)
    padded = jnp.pad(padded, ((1, 1), (0, 0), (0, 0)))
    curv = curvature_of(padded)
    return slope * (first_residual[:, None, :] + second_residual[:, :, None]) - LAMBDA * curv


def solution(mesh):
    in_specs = (
        P("slab", "bx", "by"),
        P("slab", "by"),
        P("slab", "bx"),
        P("slab", "by"),
        P("slab", "bx"),
        P(),
    )
    out_specs = P("slab", "bx", "by")
    return jax.shard_map(
        per_device, mesh=mesh, in_specs=in_specs, out_specs=out_specs, check_vma=False
    )
```

```python
import functools

import jax
import jax.numpy as jnp
from jax import lax
from jax.experimental import pallas as pl
from jax.experimental.pallas import tpu as pltpu
from jax.sharding import PartitionSpec as P

LAMBDA = 0.5
BETA2 = 1.0
TILE = 128
GROUP = 8
MESH = pl.DeviceIdType.MESH


def exchange_kernel(
    n, phi_hbm, ma_hbm, mb_hbm, va_hbm, vb_hbm, rows_hbm,
    base_hbm, ra_hbm, rb_hbm,
    ext, out, esend_recv, sums, rs_recv, pieces, ra_out, bsum, bsum_recv, rb,
    x_first, x_last, h_next, h_prev, corner, flux_prev, flux_row,
    ma, va, mb, vb, rows,
    in_sem, small_sem, out_sem, fin_sem,
    rs_send, rs_sem, ag_send, ag_sem, pair_send, pair_sem, halo_send, halo_sem,
):
    planes, cells_x, cells_y = phi_hbm.shape
    groups = planes // GROUP
    me = lax.axis_index("bx")
    half = lax.axis_index("by")
    other = 1 - half
    total_x = cells_x * n
    total_y = cells_y * 2

    barrier = pltpu.get_barrier_semaphore()
    for k in range(1, n):
        pl.semaphore_signal(barrier, inc=1, device_id={"bx": lax.rem(me + k, n)}, device_id_type=MESH)
    for k in range(n):
        pl.semaphore_signal(
            barrier, inc=1, device_id={"bx": lax.rem(me + k, n), "by": other}, device_id_type=MESH
        )

    def load(g):
        return pltpu.make_async_copy(
            phi_hbm.at[pl.ds(g * GROUP, GROUP)],
            ext.at[pl.ds(g * GROUP, GROUP), :, pl.ds(TILE, cells_y)],
            in_sem.at[g],
        )

    for g in range(groups):
        load(g).start()
    lanes_me = pl.ds(pl.multiple_of(me * TILE, TILE), TILE)
    small = [
        pltpu.make_async_copy(ma_hbm.at[:, lanes_me], ma, small_sem.at[0]),
        pltpu.make_async_copy(va_hbm.at[:, lanes_me], va, small_sem.at[1]),
        pltpu.make_async_copy(mb_hbm, mb, small_sem.at[2]),
        pltpu.make_async_copy(vb_hbm, vb, small_sem.at[3]),
        pltpu.make_async_copy(rows_hbm, rows, small_sem.at[4]),
    ]
    for copy in small:
        copy.start()

    for g in range(groups):
        load(g).wait()

        def first_pass(c, _, g=g):
            at = pl.ds(g * GROUP, GROUP)
            cells = ext[at, :, pl.ds(pl.multiple_of(TILE + c * TILE, TILE), TILE)]
            t = jnp.tanh(cells)
            sums[c, at, :] = jnp.sum(t, axis=1)
            cols = pl.ds(pl.multiple_of(c * TILE, TILE), TILE)
            x_first[at, cols] = cells[:, 0, :]
            x_last[at, cols] = cells[:, cells_x - 1, :]
            return _ + t

        bsum[pl.ds(g * GROUP, GROUP)] = lax.fori_loop(
            0, n, first_pass, jnp.zeros((GROUP, cells_x, TILE), jnp.float32)
        )

    pl.semaphore_wait(barrier, 2 * n - 1)

    def scatter(k):
        to = lax.rem(me + k, n)
        return pltpu.make_async_remote_copy(
            src_ref=sums.at[to], dst_ref=rs_recv.at[n - k], send_sem=rs_send.at[k],
            recv_sem=rs_sem.at[n - k], device_id={"bx": to}, device_id_type=MESH,
        )

    def gather(k):
        to = lax.rem(me + k, n)
        return pltpu.make_async_remote_copy(
            src_ref=pieces.at[me], dst_ref=pieces.at[me], send_sem=ag_send.at[k],
            recv_sem=ag_sem.at[n - k], device_id={"bx": to}, device_id_type=MESH,
        )

    def pair(i):
        edge = pl.ds(pl.multiple_of(TILE + other * (cells_y - TILE), TILE), TILE)
        src, dst = ((ext.at[pl.ds(0, planes), :, edge], esend_recv), (bsum, bsum_recv))[i]
        return pltpu.make_async_remote_copy(
            src_ref=src, dst_ref=dst, send_sem=pair_send.at[i], recv_sem=pair_sem.at[i],
            device_id={"by": other}, device_id_type=MESH,
        )

    def to_next():
        return pltpu.make_async_remote_copy(
            src_ref=x_last, dst_ref=h_prev, send_sem=halo_send.at[0], recv_sem=halo_sem.at[0],
            device_id={"bx": lax.rem(me + 1, n)}, device_id_type=MESH,
        )

    def to_prev():
        return pltpu.make_async_remote_copy(
            src_ref=x_first, dst_ref=h_next, send_sem=halo_send.at[1], recv_sem=halo_sem.at[1],
            device_id={"bx": lax.rem(me + n - 1, n)}, device_id_type=MESH,
        )

    def corner_prev():
        return pltpu.make_async_remote_copy(
            src_ref=x_first.at[:, pl.ds(cells_y - TILE, TILE)], dst_ref=corner,
            send_sem=halo_send.at[2], recv_sem=halo_sem.at[2],
            device_id={"bx": lax.rem(me + n - 1, n), "by": other}, device_id_type=MESH,
        )

    def corner_next():
        return pltpu.make_async_remote_copy(
            src_ref=x_last.at[:, pl.ds(0, TILE)], dst_ref=corner,
            send_sem=halo_send.at[2], recv_sem=halo_sem.at[2],
            device_id={"bx": lax.rem(me + 1, n), "by": other}, device_id_type=MESH,
        )

    has_next = me < n - 1
    has_prev = me > 0
    for k in range(1, n):
        scatter(k).start()
    for i in range(2):
        pair(i).start()

    @pl.when(has_next)
    def _():
        to_next().start()

    @pl.when(has_prev)
    def _():
        to_prev().start()

    @pl.when(jnp.logical_and(has_prev, half == 0))
    def _():
        corner_prev().start()

    @pl.when(jnp.logical_and(has_next, half == 1))
    def _():
        corner_next().start()

    def store(g):
        at = pl.ds(g * GROUP, GROUP)
        return pltpu.make_async_copy(out.at[at], base_hbm.at[at], out_sem.at[g])

    pair(0).wait_recv()
    lane3 = lax.broadcasted_iota(jnp.int32, (GROUP, cells_x, TILE), 2)
    keep3 = lane3 == half * (TILE - 1)
    for g in range(groups):
        at = pl.ds(g * GROUP, GROUP)
        ext[at, :, pl.ds(0, TILE)] = jnp.where(keep3, esend_recv[at], 0.0)
    ext[planes] = jnp.zeros((cells_x, cells_y + TILE), jnp.float32)

    width = cells_y + TILE
    row = lax.broadcasted_iota(jnp.int32, (cells_x, width), 0)

    def curvature(z, flux_z_before):
        cells = ext[z]
        right = pltpu.roll(cells, cells_x - 1, axis=0)
        gz = ext[z + 1] - cells
        gx = right - cells
        gy = pltpu.roll(cells, width - 1, axis=1) - cells
        scale = LAMBDA * lax.rsqrt(gz * gz + gx * gx + gy * gy + BETA2)
        fz = gz * scale
        fx = gx * scale
        fy = gy * scale
        fx_before = jnp.where(row == 0, 0.0, pltpu.roll(fx, 1, axis=0))
        fy_before = pltpu.roll(fy, 1, axis=1)
        div = (fz - flux_z_before) + (fx - fx_before) + (fy - fy_before)
        flux_row[pl.ds(z, 1), :] = fx[cells_x - 2:cells_x - 1, :]
        out[z] = div[:, TILE:]
        return fz

    flux_z = LAMBDA * ext[0] * lax.rsqrt(ext[0] * ext[0] + BETA2)
    flux_z = lax.fori_loop(0, planes // 2, curvature, flux_z)

    for copy in small:
        copy.wait()
    own = lax.broadcasted_iota(jnp.int32, (planes, planes), 0)
    across = lax.broadcasted_iota(jnp.int32, (planes, planes), 1)
    offsets = (rows[...] - 2 * across).astype(jnp.float32)
    odd = jnp.sum(jnp.where(own == across, offsets, 0.0), axis=1, keepdims=True) > 0.5

    def rows_of(ref):
        low = ref[pl.ds(0, planes, stride=2), :].astype(jnp.float32)
        high = ref[pl.ds(1, planes, stride=2), :].astype(jnp.float32)
        return jnp.where(odd, high, low)

    measured_a = rows_of(ma)
    mask_a = rows_of(va)
    measured_b = mb[...]
    mask_b = vb[...].astype(jnp.float32)
    detectors = mb.shape[1]
    detector = lax.broadcasted_iota(jnp.int32, (cells_x, detectors), 1).astype(jnp.float32)
    wanted = rows[...].astype(jnp.float32)

    total = sums[me]
    for k in range(1, n):
        scatter(n - k).wait_recv()
        total = total + rs_recv[k]
    pieces[me] = mask_a * ((2.0 + (2.0 / total_x) * total) - measured_a)
    for k in range(1, n):
        gather(k).start()

    lax.fori_loop(planes // 2, planes, curvature, flux_z)
    pair(1).wait_recv()

    def second_view(z, _):
        pick = detector == jnp.sum(jnp.where(across[:1] == z, wanted, 0.0), axis=1, keepdims=True)
        both = jnp.sum(bsum[z] + bsum_recv[z], axis=1, keepdims=True)
        meas = jnp.sum(jnp.where(pick, measured_b, 0.0), axis=1, keepdims=True)
        mask = jnp.sum(jnp.where(pick, mask_b, 0.0), axis=1, keepdims=True)
        res = mask * ((2.0 + (2.0 / total_y) * both) - meas)
        rb[z] = jnp.broadcast_to(res, (cells_x, TILE))
        return _

    lax.fori_loop(0, planes, second_view, 0)
    rb_copy = pltpu.make_async_copy(rb, rb_hbm, fin_sem.at[0])
    rb_copy.start()

    @pl.when(has_prev)
    def _():
        to_next().wait_recv()

    @pl.when(jnp.logical_not(has_prev))
    def _():
        h_prev[...] = jnp.zeros_like(h_prev)

    @pl.when(has_next)
    def _():
        to_prev().wait_recv()

    @pl.when(jnp.logical_not(has_next))
    def _():
        h_next[...] = jnp.zeros_like(h_next)

    has_corner = jnp.logical_or(
        jnp.logical_and(has_prev, half == 0), jnp.logical_and(has_next, half == 1)
    )

    @pl.when(has_corner)
    def _():
        corner_prev().wait_recv()

    @pl.when(jnp.logical_not(has_corner))
    def _():
        corner[...] = jnp.zeros_like(corner)

    lane2 = lax.broadcasted_iota(jnp.int32, (planes, TILE), 1)
    corners = jnp.where(lane2 == half * (TILE - 1), corner[...], 0.0)
    before = jnp.concatenate([corners, h_prev[...]], axis=1)
    first = jnp.concatenate([jnp.zeros((planes, TILE), jnp.float32), x_first[...]], axis=1)
    above = pltpu.roll(before, planes - 1, axis=0)
    level = lax.broadcasted_iota(jnp.int32, (planes, width), 0)
    gz = jnp.where(level == planes - 1, 0.0, above) - before
    gx = first - before
    gy = pltpu.roll(before, width - 1, axis=1) - before
    flux_prev[...] = LAMBDA * gx * lax.rsqrt(gz * gz + gx * gx + gy * gy + BETA2)

    edge = ext[pl.ds(0, planes), :, pl.ds(0, TILE)][:, cells_x - 1, :]
    last = jnp.concatenate([edge, x_last[...]], axis=1)
    after = jnp.concatenate([corners, h_next[...]], axis=1)
    gz = jnp.where(level == planes - 1, 0.0, pltpu.roll(last, planes - 1, axis=0)) - last
    gx = after - last
    gy = pltpu.roll(last, width - 1, axis=1) - last
    scale = LAMBDA * lax.rsqrt(gz * gz + gx * gx + gy * gy + BETA2)
    fz = gz * scale
    fy = gy * scale
    pad = LAMBDA * last * lax.rsqrt(last * last + BETA2)
    fz_before = jnp.where(level == 0, pad, pltpu.roll(fz, 1, axis=0))
    div = (fz - fz_before) + (gx * scale - flux_row[...]) + (fy - pltpu.roll(fy, 1, axis=1))
    flux_row[...] = div

    def complete(z, _):
        out[z, pl.ds(cells_x - 1, 1), :] = flux_row[pl.ds(z, 1), pl.ds(TILE, cells_y)]
        out[z, pl.ds(0, 1), :] = out[z, pl.ds(0, 1), :] - flux_prev[pl.ds(z, 1), pl.ds(TILE, cells_y)]
        return _

    lax.fori_loop(0, planes, complete, 0)
    for g in range(groups):
        store(g).start()

    for k in range(1, n):
        gather(k).wait_recv()
    for c in range(n):
        ra_out[:, c * TILE:(c + 1) * TILE] = pieces[c]
    ra_copy = pltpu.make_async_copy(ra_out, ra_hbm, fin_sem.at[1])
    ra_copy.start()

    for k in range(1, n):
        scatter(k).wait_send()
        gather(k).wait_send()
    pair(0).wait_send()
    pair(1).wait_send()

    @pl.when(has_next)
    def _():
        to_next().wait_send()

    @pl.when(has_prev)
    def _():
        to_prev().wait_send()

    @pl.when(jnp.logical_and(has_prev, half == 0))
    def _():
        corner_prev().wait_send()

    @pl.when(jnp.logical_and(has_next, half == 1))
    def _():
        corner_next().wait_send()

    for g in range(groups):
        store(g).wait()
    rb_copy.wait()
    ra_copy.wait()


def finish_kernel(phi, base, ra, rb, grad):
    planes, cells_x, cells_y = phi.shape
    for z in range(planes):
        for c in range(cells_y // TILE):
            cols = pl.ds(c * TILE, TILE)
            t = jnp.tanh(phi[z, :, cols])
            res = ra[pl.ds(z, 1), cols] + rb[z]
            grad[z, :, cols] = (0.5 - 0.5 * (t * t)) * res - base[z, :, cols]


def per_device_kernels(n, phi, ma, mb, va, vb, rows):
    planes, cells_x, cells_y = phi.shape
    f32 = jnp.float32
    dma = pltpu.SemaphoreType.DMA
    det = ma.shape[0]
    groups = planes // GROUP
    any_spec = pl.BlockSpec(memory_space=pl.ANY)
    vmem = lambda *shape: pltpu.VMEM(shape, f32)
    base, ra, rb = pl.pallas_call(
        functools.partial(exchange_kernel, n),
        out_shape=(
            jax.ShapeDtypeStruct(phi.shape, f32),
            jax.ShapeDtypeStruct((planes, cells_y), f32),
            jax.ShapeDtypeStruct((planes, cells_x, TILE), f32),
        ),
        in_specs=[pl.BlockSpec(memory_space=pltpu.HBM)] * 6,
        out_specs=(any_spec,) * 3,
        scratch_shapes=[
            vmem(planes + 1, cells_x, cells_y + TILE), vmem(planes, cells_x, cells_y),
            vmem(planes, cells_x, TILE),
            vmem(n, planes, TILE), vmem(n, planes, TILE), vmem(n, planes, TILE), vmem(planes, cells_y),
            vmem(planes, cells_x, TILE), vmem(planes, cells_x, TILE), vmem(planes, cells_x, TILE),
            vmem(planes, cells_y), vmem(planes, cells_y), vmem(planes, cells_y), vmem(planes, cells_y),
            vmem(planes, TILE), vmem(planes, cells_y + TILE), vmem(planes, cells_y + TILE),
            vmem(det, TILE), pltpu.VMEM((det, TILE), jnp.int32),
            vmem(cells_x, det), pltpu.VMEM((cells_x, det), jnp.int32),
            pltpu.VMEM((1, planes), jnp.int32),
            dma((groups,)), dma((5,)), dma((groups,)), dma((2,)),
            dma((n,)), dma((n,)), dma((n,)), dma((n,)), dma((2,)), dma((2,)), dma((3,)), dma((3,)),
        ],
        compiler_params=pltpu.CompilerParams(
            collective_id=0, has_side_effects=True, vmem_limit_bytes=24 << 20
        ),
    )(*[pltpu.with_memory_space_constraint(x, pltpu.HBM) for x in (phi, ma, mb.T, va, vb.T, rows.reshape(1, planes))])
    block = pl.BlockSpec((GROUP, cells_x, cells_y), lambda i: (i, 0, 0))
    return pl.pallas_call(
        finish_kernel,
        grid=(groups,),
        out_shape=jax.ShapeDtypeStruct(phi.shape, f32),
        in_specs=[
            block, block,
            pl.BlockSpec((GROUP, cells_y), lambda i: (i, 0)),
            pl.BlockSpec((GROUP, cells_x, TILE), lambda i: (i, 0, 0)),
        ],
        out_specs=block,
        compiler_params=pltpu.CompilerParams(vmem_limit_bytes=16 << 20),
    )(phi, base, ra, rb)


def extended(cells, sides, width):
    for axis, dim in sides:
        count = lax.axis_size(axis)
        ends = count - 1
        head = lax.slice_in_dim(cells, 0, width, axis=dim)
        tail = lax.slice_in_dim(cells, cells.shape[dim] - width, cells.shape[dim], axis=dim)
        cells = jnp.concatenate(
            [
                lax.ppermute(tail, axis, [(i, (i + 1) % count) for i in range(ends)]),
                cells,
                lax.ppermute(head, axis, [((i + 1) % count, i) for i in range(ends)]),
            ],
            axis=dim,
        )
    return cells


def curvature_of(padded):
    core = padded[:-1, :-1, :-1]
    grad_z = padded[1:, :-1, :-1] - core
    grad_x = padded[:-1, 1:, :-1] - core
    grad_y = padded[:-1, :-1, 1:] - core
    magnitude = jnp.sqrt(grad_z * grad_z + grad_x * grad_x + grad_y * grad_y + BETA2)
    flux_z = grad_z / magnitude
    flux_x = grad_x / magnitude
    flux_y = grad_y / magnitude
    div_z = flux_z[1:, 1:, 1:] - flux_z[:-1, 1:, 1:]
    div_x = flux_x[1:, 1:, 1:] - flux_x[1:, :-1, 1:]
    div_y = flux_y[1:, 1:, 1:] - flux_y[1:, 1:, :-1]
    return div_z + div_x + div_y


def per_device(
    phi,
    first_measurement,
    second_measurement,
    first_view_mask,
    second_view_mask,
    plane_detector_rows,
):
    planes, cells_x, cells_y = phi.shape
    n = lax.axis_size("bx")
    if lax.axis_size("by") == 2 and n * TILE == cells_y and planes % GROUP == 0:
        return per_device_kernels(
            n, phi, first_measurement, second_measurement, first_view_mask, second_view_mask,
            plane_detector_rows,
        )
    total_x = cells_x * lax.axis_size("bx")
    total_y = cells_y * lax.axis_size("by")
    tanh_phi = jnp.tanh(phi)
    heav = 0.5 * (1.0 + tanh_phi)
    slope = 0.5 * (1.0 - tanh_phi * tanh_phi)
    part_a = jnp.sum(heav, axis=1)
    part_b = jnp.sum(heav, axis=2)
    first_measured_rows = jnp.take(first_measurement, plane_detector_rows, axis=0)
    first_mask_rows = jnp.take(first_view_mask, plane_detector_rows, axis=0).astype(jnp.float32)
    second_measured_rows = jnp.take(second_measurement, plane_detector_rows, axis=0)
    second_mask_rows = jnp.take(second_view_mask, plane_detector_rows, axis=0).astype(jnp.float32)
    second_projection = lax.psum(part_b, "by") * (4.0 / total_y)
    second_residual = second_mask_rows * (second_projection - second_measured_rows)
    first_projection = lax.psum(part_a, "bx") * (4.0 / total_x)
    first_residual = first_mask_rows * (first_projection - first_measured_rows)
    padded = extended(phi, (("bx", 1), ("by", 2)), 1)
    padded = jnp.pad(padded, ((1, 1), (0, 0), (0, 0)))
    curv = curvature_of(padded)
    return slope * (first_residual[:, None, :] + second_residual[:, :, None]) - LAMBDA * curv


def solution(mesh):
    in_specs = (
        P("slab", "bx", "by"),
        P("slab", "by"),
        P("slab", "bx"),
        P("slab", "by"),
        P("slab", "bx"),
        P(),
    )
    out_specs = P("slab", "bx", "by")
    return jax.shard_map(
        per_device, mesh=mesh, in_specs=in_specs, out_specs=out_specs, check_vma=False
    )
```
